32 devices in a mesh: groups: 2 (over x), ctx: 16 (over z, y, core).
Axes of the slice: x: 2, y: 2, z: 4, core: 2. Of those that a mesh axis runs over, the one named last changes fastest.
Arguments:
- projected: bfloat16 [3, 16384, 4096], P(None, ('groups', 'ctx')), parts along dimension 1, may hold values from -6 to 6
- conv_weight: float32 [3, 4, 4096], replicated, may hold values from -3 to 3
- level_codes: int32 [14, 32, 16384], P(None, None, ('groups', 'ctx')), parts along dimension 2, may hold values from 1 to 16
- out_gain: float32 [4096], replicated, may hold values from 0.25 to 1.75
Outputs:
- mixed: bfloat16 [16384, 4096], P(('groups', 'ctx')), parts along dimension 0
The draws below stay inside these ranges and needn't reach their ends.
There are 2 independent parts, one for each index of `groups`. The reference program is written for one: setup_inputs(seed, part) draws one part's arguments, and reference() takes and returns one part's arrays. A program takes and returns all parts, laid end to end along the dimension named above; an argument that names none is the same for every part. Nothing has to cross between parts.
Inputs may be any that keep to these rules, and one draw needn't show every extreme that they name: `level_codes`: numerators of the level coefficients, which are the values divided by 8.
All inputs are finite; a program needn't handle non-finite values.
Results may differ from the reference program's by a relative error of at most 0.007.
Values may be sent and summed in bfloat16 or wider, within the bound.
A program may use at most 192 MiB of HBM per device.

```python
import jax
import jax.numpy as jnp
from jax import lax

H = 32
DH = 128
D = 4096
KW = 4
TOK_DEV = 512
TOK_BITS = 9
CTX_BITS = 4
LEVELS = 14
TOKENS = 8192
N_CTX = 16


def touch_ends(array, key, smallest, high):
    dims = array.shape
    index_at = [jax.random.randint(jax.random.fold_in(key, axis), (), 0, dims[axis]) for axis in range(len(dims))]
    array = array.at[tuple(index_at)].set(smallest)
    longest = dims.index(max(dims))
    index_at[longest] = (index_at[longest] + 1) % dims[longest]
    return array.at[tuple(index_at)].set(high)


def levels(key, shape, pieces, least, high):
    factor_of, own = 1.0, jax.random.fold_in(key, 6)
    for dim, shards_of in pieces:
        draws = jnp.exp(jax.random.uniform(jax.random.fold_in(own, dim), (shards_of,), jnp.float32, least / len(pieces), high / len(pieces)))
        factor_of = factor_of * jnp.repeat(draws, shape[dim] // shards_of).reshape([-1 if axis == dim else 1 for axis in range(len(shape))])
    return factor_of


def noise(stream_key, dims, spread, limit, split=(), dtype=jnp.bfloat16):
    result = jax.random.normal(stream_key, dims, jnp.float32) * spread
    if len(split) > 0:
        result = levels(stream_key, dims, split, -0.22, 0.18) * result
    return jnp.clip(result, min=-limit, max=limit).astype(dtype)


def setup_inputs(seed: int = 0, part: int = 0) -> dict:
    splits = jax.random.split(jax.random.key(seed), 5)
    own_keys = jax.random.split(jax.random.fold_in(splits[4], part), 5)
    return {
        "projected": noise(own_keys[0], (3, TOKENS, D), 1.0, 6.0, ((1, 16),)),
        "conv_weight": noise(splits[1], (3, KW, D), 0.5, 3.0, (), jnp.float32),
        "level_codes": touch_ends(jax.random.randint(own_keys[2], (LEVELS, H, TOKENS), 1, 17), jax.random.fold_in(own_keys[2], 1), 1, 16).astype(jnp.int32),
        "out_gain": jnp.clip(1.0 + 0.15 * jax.random.normal(splits[3], (D,), jnp.float32), 0.25, 1.75),
    }


def convolve(projected, conv_weight):
    tap_count = conv_weight.shape[1]
    row_count = projected.shape[1]
    source = projected.astype(jnp.float32)
    padded = jnp.concatenate([jnp.zeros((3, tap_count - 1, source.shape[2]), jnp.float32), source], 1)
    running = jnp.zeros(source.shape, jnp.float32)
    for offset in range(tap_count):
        running = running + conv_weight[:, offset, None, :] * padded[:, offset:offset + row_count, :]
    return running.astype(jnp.bfloat16)

def intra_levels(length, bit_count):
    position = lax.iota(jnp.int32, length)
    differ = jnp.bitwise_xor(position[:, None], position[None, :])
    level = jnp.zeros((length, length), jnp.int32)
    for exponent in range(bit_count):
        level = level + (differ >= 2 ** exponent).astype(jnp.int32)
    causal = position[None, :] <= position[:, None]
    return jnp.stack([(causal & (level == number)).astype(jnp.float32) for number in range(bit_count + 1)])

def local_layer(query_rows, key_rows, value_rows, level_weight, fenwick, onehot, out_gain):
    highest = lax.Precision.HIGHEST
    scores = jnp.einsum('thd,shd->hts', query_rows, key_rows, precision=highest)
    weight = jnp.einsum('lts,lht->hts', onehot, level_weight[:TOK_BITS + 1], precision=highest)
    weights = lax.optimization_barrier((scores * weight).astype(jnp.bfloat16)).astype(jnp.float32)
    inside = jnp.einsum('hts,shd->thd', weights, value_rows, precision=highest)
    fenwick_bf = lax.optimization_barrier(fenwick.astype(jnp.bfloat16)).astype(jnp.float32)
    across = jnp.zeros(inside.shape, jnp.float32)
    for bit_index in range(CTX_BITS):
        product = jnp.einsum('thd,hde->the', query_rows, fenwick_bf[bit_index], precision=highest)
        across = across + level_weight[TOK_BITS + 1 + bit_index].T[:, :, None] * product
    combined = inside + across
    inverse = lax.rsqrt(lax.optimization_barrier(jnp.mean(combined * combined, -1, keepdims=True)) + 1e-06)
    normed = combined * inverse * out_gain.reshape(H, DH)
    return normed.astype(jnp.bfloat16).reshape(TOK_DEV, H * DH)

def reference(projected, conv_weight, level_codes, out_gain):
    mixed_in = convolve(projected, conv_weight)
    level_weight = level_codes.astype(jnp.float32) / 8.0
    onehot = intra_levels(TOK_DEV, TOK_BITS)
    heads_all = mixed_in.reshape(3, N_CTX, TOK_DEV, H, DH).astype(jnp.float32)
    states = jnp.einsum('cshd,cshe->chde', heads_all[1], heads_all[2], precision=lax.Precision.HIGHEST)
    span_ids = lax.iota(jnp.int32, N_CTX)
    differ = jnp.bitwise_xor(span_ids[:, None], span_ids[None, :])
    earlier = span_ids[None, :] < span_ids[:, None]
    bucket_masks = jnp.stack([(earlier & (differ >= 2 ** bit_index) & (differ < 2 ** (bit_index + 1))).astype(jnp.float32) for bit_index in range(CTX_BITS)])
    outputs = []
    for span_index in range(N_CTX):
        fenwick = jnp.einsum('bs,shde->bhde', bucket_masks[:, span_index, :], states, precision=lax.Precision.HIGHEST)
        level_part = level_weight[:, :, span_index * TOK_DEV:(span_index + 1) * TOK_DEV]
        outputs.append(local_layer(heads_all[0, span_index], heads_all[1, span_index], heads_all[2, span_index], level_part, fenwick, onehot, out_gain))
    return jnp.concatenate(outputs, 0)
```

```python
import functools

import jax
import jax.numpy as jnp
from jax import lax
from jax.experimental import pallas as pl
from jax.experimental.pallas import tpu as pltpu
from jax.sharding import PartitionSpec as P

PAD = 8
TILE = 128
MESH = pl.DeviceIdType.MESH
F32, BF16 = jnp.float32, jnp.bfloat16
LAG = {0: 2, 1: 6, 2: 10}
LAST = (5, 3, 2)


def spread(count, dim):
    bits = count.bit_length() - 1
    depth = [0] + [1] * (bits - 2) + [min(2, bits - 1)] if bits > 1 else [0]
    swaps = [("swap", bit, 0) for bit in range(bits)]
    shares = [("share", bit, at) for bit in range(bits) for at in reversed(range(depth[bit]))]
    return bits, depth, swaps + shares


def kernel(sizes, *refs):
    heads, dim, rows, taps, level_count, count, chunk, group = sizes
    bits, depth, moves = spread(count, dim)
    chunks = heads // chunk
    width = heads * dim
    tok_bits = rows.bit_length() - 1
    block = min(2 * TILE, rows)
    blocks = rows // block
    block_bits = blocks.bit_length() - 1
    top = TILE.bit_length() - 1
    strip = PAD.bit_length() - 1
    nodes = [(bit, at) for bit in range(block_bits) for at in range(0, blocks >> bit, 2)]

    projected, conv_weight, codes, gain, out = refs[:5]
    xs, taps_in, code_in, lam, gains, rim, held, outer = refs[5:13]
    keys, values_t, queries_t, inner, within, mixed, state = refs[13:20]
    accs = [state] + list(refs[20 : 20 + bits - 1])
    gots = refs[19 + bits : 19 + 2 * bits]
    send_sem, recv_sem, rim_send, rim_recv, small_sem, kv_sem, q_sem, out_sem = refs[19 + 2 * bits :]

    part = lax.axis_index("groups")
    me = lax.axis_index("ctx")

    def region(level):
        start = 0
        for step in range(level):
            start = start + ((me >> step) & 1) * (dim >> (step + 1))
        return pl.ds(pl.multiple_of(start, dim >> level), dim >> level)

    def transfer(move, g):
        kind, bit, at = moves[move]
        which = pl.ds(g * chunk, chunk)
        if kind == "swap":
            source, target = accs[bit].at[which], gots[bit].at[which, region(depth[bit])]
            to = me ^ (1 << bit)
        else:
            source = target = gots[bit].at[which, region(at + 1)]
            to = me ^ (1 << at)
        return pltpu.make_async_remote_copy(
            src_ref=source,
            dst_ref=target,
            send_sem=send_sem.at[move, g],
            recv_sem=recv_sem.at[move, g],
            device_id=(part, to),
            device_id_type=MESH,
        )

    def small(index):
        pair = [(conv_weight, taps_in), (codes, code_in), (gain, gains)][index]
        return pltpu.make_async_copy(*pair, small_sem.at[index])

    def load(kind, g, sem):
        lanes = pl.ds(g * group * dim, group * dim)
        return pltpu.make_async_copy(projected.at[kind, :, lanes], xs.at[kind, :, lanes], sem)

    def load_kv(g):
        lanes = pl.ds(pl.multiple_of(g * group * dim, group * dim), group * dim)
        return pltpu.make_async_copy(
            projected.at[pl.ds(1, 2), :, lanes], xs.at[pl.ds(1, 2), :, lanes], kv_sem.at[g]
        )

    def load_q(g):
        lanes = pl.ds(pl.multiple_of(g * group * dim, group * dim), group * dim)
        return pltpu.make_async_copy(projected.at[0, :, lanes], xs.at[0, :, lanes], q_sem.at[g])

    def rim_copy(index):
        kinds = [pl.ds(1, 2), pl.ds(0, 1)][index]
        return pltpu.make_async_remote_copy(
            src_ref=projected.at[kinds, pl.ds(rows - PAD, PAD)],
            dst_ref=rim.at[kinds],
            send_sem=rim_send.at[index],
            recv_sem=rim_recv.at[index],
            device_id=(part, me + 1),
            device_id_type=MESH,
        )

    for index in range(3):
        small(index).start()
    for g in range(heads // group):
        load_kv(g).start()
    for g in range(heads // group):
        load_q(g).start()

    barrier = pltpu.get_barrier_semaphore()
    for bit in range(bits):
        pl.semaphore_signal(barrier, inc=1, device_id=(part, me ^ (1 << bit)), device_id_type=MESH)
    odd = me & 1
    beside = me + 2 * odd - 1
    has_beside = (beside >= 0) & (beside < count)

    @pl.when(has_beside)
    def _():
        pl.semaphore_signal(barrier, inc=1, device_id=(part, beside), device_id_type=MESH)

    pl.semaphore_wait(barrier, bits + jnp.where(has_beside, 1, 0))

    @pl.when(me < count - 1)
    def _():
        rim_copy(0).start()
        rim_copy(1).start()

    @pl.when(me == 0)
    def _():
        rim[...] = jnp.zeros_like(rim)

    for index in range(3):
        small(index).wait()
    for level in range(level_count):
        scale = 0.125
        if level > tok_bits:
            scale = ((me >> (level - tok_bits - 1)) & 1).astype(F32) * 0.125
        for tile in range(rows // TILE):
            lanes = slice(tile * TILE, (tile + 1) * TILE)
            lam[level, tile] = code_in[level, :, lanes].astype(F32) * scale

    @pl.when(me > 0)
    def _():
        rim_copy(0).wait_recv()
        rim_copy(1).wait_recv()

    def convolve(kind, head, slot):
        lanes = pl.ds(pl.multiple_of(head * dim, dim), dim)
        line = held.at[slot]
        line[0:PAD, :] = rim[kind, :, lanes].astype(F32)
        own = xs[kind, :, lanes].astype(F32)
        line[PAD : PAD + rows, :] = own
        total = taps_in[kind, taps - 1 : taps, lanes] * own
        for tap in range(taps - 1):
            first = PAD - taps + 1 + tap
            total = total + taps_in[kind, tap : tap + 1, lanes] * line[first : first + rows, :]
        return total.astype(BF16)

    def states(g):
        for index in range(chunk):
            head = g * chunk + index
            key = convolve(1, head, 2 * index)
            keys[head] = key
            value_t = convolve(2, head, 2 * index + 1).T
            values_t[head] = value_t
            sums = []
            for at in range(blocks):
                span = slice(at * block, (at + 1) * block)
                sums.append(jnp.dot(value_t[:, span], key[span], preferred_element_type=F32))
            for number, (bit, at) in enumerate(nodes):
                inner[number, head] = sum(sums[at << bit : (at + 1) << bit]).astype(BF16)
            state[head] = sum(sums).astype(BF16)

    strips = TILE // PAD
    lane8 = lax.broadcasted_iota(jnp.int32, (PAD, TILE), 1)
    row8 = lax.broadcasted_iota(jnp.int32, (PAD, TILE), 0)
    lane_strip = lax.broadcasted_iota(jnp.int32, (strips, TILE), 1) >> strip
    row_strip = lax.broadcasted_iota(jnp.int32, (strips, TILE), 0)

    def lam_row(level, head, span):
        tiles = range(span.start // TILE, span.stop // TILE)
        return jnp.concatenate([lam[level, tile, pl.ds(head, 1), :] for tile in tiles], 1)

    def diagonal(head, tile):
        span = slice(tile * TILE, (tile + 1) * TILE)
        differ = lane_strip ^ row_strip
        wide = jnp.broadcast_to(lam_row(top, head, span), differ.shape)
        for level in range(top - 1, strip, -1):
            wide = jnp.where(differ < 2 ** (level - strip), lam_row(level, head, span), wide)
        outer[:, span] = jnp.where(row_strip <= lane_strip, wide, 0.0)
        differ8 = (lane8 & (PAD - 1)) ^ row8
        near = jnp.broadcast_to(lam_row(strip, head, span), differ8.shape)
        for level in range(strip - 1, -1, -1):
            near = jnp.where(differ8 < 2**level, lam_row(level, head, span), near)
        near = jnp.where(row8 <= (lane8 & (PAD - 1)), near, 0.0)
        own = lane8 >> strip
        return jnp.concatenate(
            [jnp.where(own == number, near, outer[number : number + 1, span]) for number in range(strips)], 0
        )

    def inside(head):
        query_t = convolve(0, head, 2 * chunk).T
        queries_t[head] = query_t
        for at in range(blocks):
            span = slice(at * block, (at + 1) * block)
            scores = jnp.dot(keys[head, span, :], query_t[:, span], preferred_element_type=F32)
            tiles = block // TILE
            columns = []
            for tile in range(tiles):
                place = at * tiles + tile
                lanes = slice(tile * TILE, (tile + 1) * TILE)
                pieces = []
                for other in range(tiles):
                    score = scores[other * TILE : (other + 1) * TILE, lanes]
                    if other > tile:
                        pieces.append(jnp.zeros((TILE, TILE), BF16))
                        continue
                    if other == tile:
                        factor = diagonal(head, place)
                    else:
                        level = top + (other ^ tile).bit_length()
                        factor = lam_row(level, head, slice(place * TILE, (place + 1) * TILE))
                    pieces.append((score * factor).astype(BF16))
                columns.append(jnp.concatenate(pieces, 0))
            left = [values_t[head, :, span]]
            right = [jnp.concatenate(columns, 1)]
            for bit in range(block_bits):
                if at >> bit & 1:
                    node = nodes.index((bit, (at >> bit) - 1))
                    level = block.bit_length() + bit
                    scaled = query_t[:, span].astype(F32) * lam_row(level, head, span)
                    left.append(inner[node, head])
                    right.append(scaled.astype(BF16))
            within[head, :, span] = jnp.dot(
                jnp.concatenate(left, 1), jnp.concatenate(right, 0), preferred_element_type=F32
            )

    def mix(g):
        for index in range(chunk):
            head = g * chunk + index
            lanes = pl.ds(pl.multiple_of(head * dim, dim), dim)
            query_t = queries_t[head].astype(F32)
            right = [
                (query_t * lam_row(tok_bits + 1 + bit, head, slice(0, rows))).astype(BF16)
                for bit in range(bits)
            ]
            left = [gots[bit][head] for bit in range(bits)]
            total = within[head] + jnp.dot(
                jnp.concatenate(left, 1), jnp.concatenate(right, 0), preferred_element_type=F32
            )
            inverse = lax.rsqrt(jnp.mean(total * total, 0, keepdims=True) + 1e-06)
            mixed[:, lanes] = ((total * inverse).T * gains[0:1, lanes]).astype(BF16)

    def store(g):
        lanes = pl.ds(pl.multiple_of(g * chunk * dim, chunk * dim), chunk * dim)
        return pltpu.make_async_copy(mixed.at[:, lanes], out.at[:, lanes], out_sem.at[g])

    lag, at = {}, 0
    for bit in range(bits):
        at += 2 if bit == 0 else 4 if bit < bits - 1 else LAST[0]
        lag[bit] = at
    for move in range(bits, len(moves)):
        _, bit, place = moves[move]
        if bit == bits - 1 and place:
            at += LAST[1]
            lag[move] = at
    finish = max(at + LAST[2], heads - chunks)

    def handle(move, g):
        kind, bit, place = moves[move]
        transfer(move, g).wait_recv()
        if kind == "swap":
            if bit < bits - 1:
                which = pl.ds(g * chunk, chunk)
                size = dim >> depth[bit + 1]
                mine = region(depth[bit + 1])
                if depth[bit + 1] == depth[bit]:
                    old = accs[bit][which]
                else:
                    start = 0
                    for step in range(depth[bit], depth[bit + 1]):
                        start = start + ((me >> step) & 1) * (dim >> (step + 1))
                    old = accs[bit][which, pl.ds(pl.multiple_of(start, size), size), :]
                total = old.astype(F32) + gots[bit][which, mine, :].astype(F32)
                accs[bit + 1][which] = total.astype(BF16)
                transfer(bit + 1, g).start()
            if depth[bit]:
                transfer(moves.index(("share", bit, depth[bit] - 1)), g).start()
        else:
            transfer(moves.index(("share", bit, place - 1)), g).start()

    ordered = sorted(lag, key=lambda move: -lag[move])
    final = [move for move in range(len(moves)) if move not in lag]
    gate = group // chunk

    def step(t, carry):
        @pl.when(t < chunks)
        def _():
            @pl.when(lax.rem(t, gate) == 0)
            def _():
                load_kv(t // gate).wait()

            states(t)
            transfer(0, t).start()

        for move in ordered:
            g = t - lag[move]

            @pl.when((g >= 0) & (g < chunks))
            def _(move=move, g=g):
                handle(move, g)

        @pl.when(t < heads)
        def _():
            @pl.when(lax.rem(t, group) == 0)
            def _():
                load_q(t // group).wait()

            inside(t)

        @pl.when((t >= finish) & (t - finish < chunks))
        def _():
            g = t - finish
            for move in final:
                transfer(move, g).wait_recv()
            mix(g)
            store(g).start()

        return carry

    lax.fori_loop(0, finish + chunks, step, 0)

    def drain(g, carry):
        for move in range(len(moves)):
            transfer(move, g).wait_send()
        store(g).wait()
        return carry

    lax.fori_loop(0, chunks, drain, 0)

    @pl.when(me < count - 1)
    def _():
        rim_copy(0).wait_send()
        rim_copy(1).wait_send()


def on_device(projected, conv_weight, level_codes, out_gain):
    kinds, rows, width = projected.shape
    taps = conv_weight.shape[1]
    level_count, heads = level_codes.shape[:2]
    dim = width // heads
    count = lax.axis_size("ctx")
    chunk, group = 2, 4
    chunks = heads // chunk
    bits, depth, moves = spread(count, dim)
    block = min(2 * TILE, rows)
    nodes = max(1, rows // block - 1)
    sizes = (heads, dim, rows, taps, level_count, count, chunk, group)
    vmem, dma = pltpu.VMEM, pltpu.SemaphoreType.DMA
    scratch = [
        vmem((kinds, rows, width), BF16),
        vmem(conv_weight.shape, F32),
        vmem((level_count, heads, rows), jnp.int32),
        vmem((level_count, rows // TILE, heads, TILE), F32),
        vmem((1, width), F32),
        vmem((kinds, PAD, width), BF16),
        vmem((2 * chunk + 1, PAD + rows, dim), F32),
        vmem((TILE // PAD, rows), F32),
        vmem((heads, rows, dim), BF16),
        vmem((heads, dim, rows), BF16),
        vmem((heads, dim, rows), BF16),
        vmem((nodes, heads, dim, dim), BF16),
        vmem((heads, dim, rows), F32),
        vmem((rows, width), BF16),
        vmem((heads, dim, dim), BF16),
    ]
    scratch += [vmem((heads, dim >> depth[bit], dim), BF16) for bit in range(1, bits)]
    scratch += [vmem((heads, dim, dim), BF16) for _ in range(bits)]
    scratch += [
        dma((len(moves), chunks)),
        dma((len(moves), chunks)),
        dma((2,)),
        dma((2,)),
        dma((3,)),
        dma((heads // group,)),
        dma((heads // group,)),
        dma((chunks,)),
    ]
    anywhere = pl.BlockSpec(memory_space=pl.ANY)
    return pl.pallas_call(
        functools.partial(kernel, sizes),
        in_specs=[anywhere] * 4,
        out_specs=anywhere,
        out_shape=jax.ShapeDtypeStruct((rows, width), BF16),
        scratch_shapes=scratch,
        compiler_params=pltpu.CompilerParams(
            collective_id=0, has_side_effects=True, vmem_limit_bytes=63 * 2**20
        ),
        name="attend",
    )(projected, conv_weight, level_codes, out_gain.reshape(1, width))


def solution(mesh):
    placed = (P(None, ("groups", "ctx"), None), P(), P(None, None, ("groups", "ctx")), P())
    return jax.shard_map(
        on_device, mesh=mesh, in_specs=placed, out_specs=P(("groups", "ctx"), None), check_vma=False
    )
```

```python
import functools

import jax
import jax.numpy as jnp
from jax import lax
from jax.experimental import pallas as pl
from jax.experimental.pallas import tpu as pltpu
from jax.sharding import PartitionSpec as P

PAD = 8
TILE = 128
MESH = pl.DeviceIdType.MESH
F32, BF16 = jnp.float32, jnp.bfloat16
AHEAD = 2
LAST = (5, 3, 2)


def spread(count, dim):
    bits = count.bit_length() - 1
    depth = [0] + [1] * (bits - 2) + [min(2, bits - 1)] if bits > 1 else [0]
    swaps = [("swap", bit, 0) for bit in range(bits)]
    shares = [("share", bit, at) for bit in range(bits) for at in reversed(range(depth[bit]))]
    return bits, depth, swaps + shares


def kernel(sizes, *refs):
    heads, dim, rows, taps, level_count, count, chunk, group = sizes
    bits, depth, moves = spread(count, dim)
    chunks = heads // chunk
    width = heads * dim
    tok_bits = rows.bit_length() - 1
    block = min(2 * TILE, rows)
    blocks = rows // block
    block_bits = blocks.bit_length() - 1
    top = TILE.bit_length() - 1
    strip = PAD.bit_length() - 1
    nodes = [(bit, at) for bit in range(block_bits) for at in range(0, blocks >> bit, 2)]

    projected, conv_weight, codes, gain, mixed = refs[:5]
    xs, taps_in, code_in, lam, gains, rim, held, outer = refs[5:13]
    keys, values_t, queries_t, inner, within, state = refs[13:19]
    accs = [state] + list(refs[19 : 19 + bits - 1])
    gots = refs[18 + bits : 18 + 2 * bits]
    send_sem, recv_sem, rim_send, rim_recv, small_sem, kv_sem, q_sem = refs[18 + 2 * bits :]

    part = lax.axis_index("groups")
    me = lax.axis_index("ctx")

    def region(level):
        start = 0
        for step in range(level):
            start = start + ((me >> step) & 1) * (dim >> (step + 1))
        return pl.ds(pl.multiple_of(start, dim >> level), dim >> level)

    def transfer(move, g):
        kind, bit, at = moves[move]
        which = pl.ds(g * chunk, chunk)
        if kind == "swap":
            source, target = accs[bit].at[which], gots[bit].at[which, region(depth[bit])]
            to = me ^ (1 << bit)
        else:
            source = target = gots[bit].at[which, region(at + 1)]
            to = me ^ (1 << at)
        return pltpu.make_async_remote_copy(
            src_ref=source,
            dst_ref=target,
            send_sem=send_sem.at[move, g],
            recv_sem=recv_sem.at[move, g],
            device_id=(part, to),
            device_id_type=MESH,
        )

    def small(index):
        pair = [(conv_weight, taps_in), (codes, code_in), (gain, gains)][index]
        return pltpu.make_async_copy(*pair, small_sem.at[index])

    def load(kind, g, sem):
        lanes = pl.ds(g * group * dim, group * dim)
        return pltpu.make_async_copy(projected.at[kind, :, lanes], xs.at[kind, :, lanes], sem)

    def load_kv(g):
        lanes = pl.ds(pl.multiple_of(g * group * dim, group * dim), group * dim)
        return pltpu.make_async_copy(
            projected.at[pl.ds(1, 2), :, lanes], xs.at[pl.ds(1, 2), :, lanes], kv_sem.at[g]
        )

    def load_q(g):
        lanes = pl.ds(pl.multiple_of(g * group * dim, group * dim), group * dim)
        return pltpu.make_async_copy(projected.at[0, :, lanes], xs.at[0, :, lanes], q_sem.at[g])

    def rim_copy(index):
        first = group * dim
        lanes = [pl.ds(0, first), pl.ds(first, width - first)][index]
        return pltpu.make_async_remote_copy(
            src_ref=projected.at[:, pl.ds(rows - PAD, PAD), lanes],
            dst_ref=rim.at[:, :, lanes],
            send_sem=rim_send.at[index],
            recv_sem=rim_recv.at[index],
            device_id=(part, me + 1),
            device_id_type=MESH,
        )

    for index in range(3):
        small(index).start()
    for g in range(heads // group):
        load_kv(g).start()
    for g in range(heads // group):
        load_q(g).start()

    barrier = pltpu.get_barrier_semaphore()
    for bit in range(bits):
        pl.semaphore_signal(barrier, inc=1, device_id=(part, me ^ (1 << bit)), device_id_type=MESH)
    odd = me & 1
    beside = me + 2 * odd - 1
    has_beside = (beside >= 0) & (beside < count)

    @pl.when(has_beside)
    def _():
        pl.semaphore_signal(barrier, inc=1, device_id=(part, beside), device_id_type=MESH)

    pl.semaphore_wait(barrier, bits + jnp.where(has_beside, 1, 0))

    @pl.when(me < count - 1)
    def _():
        rim_copy(0).start()
        rim_copy(1).start()

    @pl.when(me == 0)
    def _():
        rim[...] = jnp.zeros_like(rim)

    for index in range(3):
        small(index).wait()
    for level in range(level_count):
        scale = 0.125
        if level > tok_bits:
            scale = ((me >> (level - tok_bits - 1)) & 1).astype(F32) * 0.125
        for tile in range(rows // TILE):
            lanes = slice(tile * TILE, (tile + 1) * TILE)
            lam[level, tile] = code_in[level, :, lanes].astype(F32) * scale

    @pl.when(me > 0)
    def _():
        rim_copy(0).wait_recv()

    def convolve(kind, head, slot):
        lanes = pl.ds(pl.multiple_of(head * dim, dim), dim)
        line = held.at[slot]
        line[0:PAD, :] = rim[kind, :, lanes].astype(F32)
        own = xs[kind, :, lanes].astype(F32)
        line[PAD : PAD + rows, :] = own
        total = taps_in[kind, taps - 1 : taps, lanes] * own
        for tap in range(taps - 1):
            first = PAD - taps + 1 + tap
            total = total + taps_in[kind, tap : tap + 1, lanes] * line[first : first + rows, :]
        return total.astype(BF16)

    def states(g):
        for index in range(chunk):
            head = g * chunk + index
            key = convolve(1, head, 2 * index)
            keys[head] = key
            value_t = convolve(2, head, 2 * index + 1).T
            values_t[head] = value_t
            sums = []
            for at in range(blocks):
                span = slice(at * block, (at + 1) * block)
                sums.append(jnp.dot(value_t[:, span], key[span], preferred_element_type=F32))
            for number, (bit, at) in enumerate(nodes):
                inner[number, head] = sum(sums[at << bit : (at + 1) << bit]).astype(BF16)
            state[head] = sum(sums).astype(BF16)

    strips = TILE // PAD
    lane8 = lax.broadcasted_iota(jnp.int32, (PAD, TILE), 1)
    row8 = lax.broadcasted_iota(jnp.int32, (PAD, TILE), 0)
    lane_strip = lax.broadcasted_iota(jnp.int32, (strips, TILE), 1) >> strip
    row_strip = lax.broadcasted_iota(jnp.int32, (strips, TILE), 0)

    def lam_row(level, head, span):
        tiles = range(span.start // TILE, span.stop // TILE)
        return jnp.concatenate([lam[level, tile, pl.ds(head, 1), :] for tile in tiles], 1)

    def diagonal(head, tile, slot):
        span = slice(tile * TILE, (tile + 1) * TILE)
        differ = lane_strip ^ row_strip
        wide = jnp.broadcast_to(lam_row(top, head, span), differ.shape)
        for level in range(top - 1, strip, -1):
            wide = jnp.where(differ < 2 ** (level - strip), lam_row(level, head, span), wide)
        outer[slot, :, span] = jnp.where(row_strip <= lane_strip, wide, 0.0)
        differ8 = (lane8 & (PAD - 1)) ^ row8
        near = jnp.broadcast_to(lam_row(strip, head, span), differ8.shape)
        for level in range(strip - 1, -1, -1):
            near = jnp.where(differ8 < 2**level, lam_row(level, head, span), near)
        near = jnp.where(row8 <= (lane8 & (PAD - 1)), near, 0.0)
        own = lane8 >> strip
        return jnp.concatenate(
            [jnp.where(own == number, near, outer[slot, number : number + 1, span]) for number in range(strips)], 0
        )

    def inside(head, slot):
        query_t = convolve(0, head, 2 * chunk + slot).T
        queries_t[head] = query_t
        for at in range(blocks):
            span = slice(at * block, (at + 1) * block)
            scores = jnp.dot(keys[head, span, :], query_t[:, span], preferred_element_type=F32)
            tiles = block // TILE
            columns = []
            for tile in range(tiles):
                place = at * tiles + tile
                lanes = slice(tile * TILE, (tile + 1) * TILE)
                pieces = []
                for other in range(tiles):
                    score = scores[other * TILE : (other + 1) * TILE, lanes]
                    if other > tile:
                        pieces.append(jnp.zeros((TILE, TILE), BF16))
                        continue
                    if other == tile:
                        factor = diagonal(head, place, slot)
                    else:
                        level = top + (other ^ tile).bit_length()
                        factor = lam_row(level, head, slice(place * TILE, (place + 1) * TILE))
                    pieces.append((score * factor).astype(BF16))
                columns.append(jnp.concatenate(pieces, 0))
            left = [values_t[head, :, span]]
            right = [jnp.concatenate(columns, 1)]
            for bit in range(block_bits):
                if at >> bit & 1:
                    node = nodes.index((bit, (at >> bit) - 1))
                    level = block.bit_length() + bit
                    scaled = query_t[:, span].astype(F32) * lam_row(level, head, span)
                    left.append(inner[node, head])
                    right.append(scaled.astype(BF16))
            within[head, :, span] = jnp.dot(
                jnp.concatenate(left, 1), jnp.concatenate(right, 0), preferred_element_type=F32
            )

    def mix(g):
        for index in range(chunk):
            head = g * chunk + index
            lanes = pl.ds(pl.multiple_of(head * dim, dim), dim)
            query_t = queries_t[head].astype(F32)
            right = [
                (query_t * lam_row(tok_bits + 1 + bit, head, slice(0, rows))).astype(BF16)
                for bit in range(bits)
            ]
            left = [gots[bit][head] for bit in range(bits)]
            total = within[head] + jnp.dot(
                jnp.concatenate(left, 1), jnp.concatenate(right, 0), preferred_element_type=F32
            )
            inverse = lax.rsqrt(jnp.mean(total * total, 0, keepdims=True) + 1e-06)
            mixed[:, lanes] = ((total * inverse).T * gains[0:1, lanes]).astype(BF16)

    lag, at = {}, -AHEAD
    for bit in range(bits):
        at += 2 if bit == 0 else 4 if bit < bits - 1 else LAST[0]
        lag[bit] = at
    for move in range(bits, len(moves)):
        _, bit, place = moves[move]
        if bit == bits - 1 and place:
            at += LAST[1]
            lag[move] = at
    finish = max(at + LAST[2], 1)

    def handle(move, g):
        kind, bit, place = moves[move]
        transfer(move, g).wait_recv()
        if kind == "swap":
            if bit < bits - 1:
                which = pl.ds(g * chunk, chunk)
                size = dim >> depth[bit + 1]
                mine = region(depth[bit + 1])
                if depth[bit + 1] == depth[bit]:
                    old = accs[bit][which]
                else:
                    start = 0
                    for step in range(depth[bit], depth[bit + 1]):
                        start = start + ((me >> step) & 1) * (dim >> (step + 1))
                    old = accs[bit][which, pl.ds(pl.multiple_of(start, size), size), :]
                total = old.astype(F32) + gots[bit][which, mine, :].astype(F32)
                accs[bit + 1][which] = total.astype(BF16)
                transfer(bit + 1, g).start()
            if depth[bit]:
                transfer(moves.index(("share", bit, depth[bit] - 1)), g).start()
        else:
            transfer(moves.index(("share", bit, place - 1)), g).start()

    ordered = sorted(lag, key=lambda move: -lag[move])
    final = [move for move in range(len(moves)) if move not in lag]
    gate = group // chunk

    def fetch(g, load):
        @pl.when(lax.rem(g, gate) == 0)
        def _():
            load(g // gate).wait()

    def inside_of(g):
        for index in range(chunk):
            inside(g * chunk + index, index)

    def early(t, carry):
        fetch(t, load_kv)
        states(t)
        transfer(0, t).start()
        return carry

    lax.fori_loop(0, AHEAD, early, 0)

    @pl.when(me > 0)
    def _():
        rim_copy(1).wait_recv()

    def step(t, carry):
        for move in ordered:
            g = t - lag[move]

            @pl.when((g >= 0) & (g < chunks))
            def _(move=move, g=g):
                handle(move, g)

        @pl.when(t < chunks)
        def _():
            fetch(t, load_q)

        @pl.when(t < chunks - AHEAD)
        def _():
            fetch(t + AHEAD, load_kv)
            states(t + AHEAD)
            inside_of(t)
            transfer(0, t + AHEAD).start()

        @pl.when((t >= chunks - AHEAD) & (t < chunks))
        def _():
            inside_of(t)

        @pl.when((t >= finish) & (t - finish < chunks))
        def _():
            g = t - finish
            for move in final:
                transfer(move, g).wait_recv()
            mix(g)

        return carry

    lax.fori_loop(0, finish + chunks, step, 0)

    def drain(g, carry):
        for move in range(len(moves)):
            transfer(move, g).wait_send()
        return carry

    lax.fori_loop(0, chunks, drain, 0)

    @pl.when(me < count - 1)
    def _():
        rim_copy(0).wait_send()
        rim_copy(1).wait_send()


def on_device(projected, conv_weight, level_codes, out_gain):
    kinds, rows, width = projected.shape
    taps = conv_weight.shape[1]
    level_count, heads = level_codes.shape[:2]
    dim = width // heads
    count = lax.axis_size("ctx")
    chunk, group = 2, 4
    chunks = heads // chunk
    bits, depth, moves = spread(count, dim)
    block = min(2 * TILE, rows)
    nodes = max(1, rows // block - 1)
    sizes = (heads, dim, rows, taps, level_count, count, chunk, group)
    vmem, dma = pltpu.VMEM, pltpu.SemaphoreType.DMA
    scratch = [
        vmem((kinds, rows, width), BF16),
        vmem(conv_weight.shape, F32),
        vmem((level_count, heads, rows), jnp.int32),
        vmem((level_count, rows // TILE, heads, TILE), F32),
        vmem((1, width), F32),
        vmem((kinds, PAD, width), BF16),
        vmem((3 * chunk, PAD + rows, dim), F32),
        vmem((chunk, TILE // PAD, rows), F32),
        vmem((heads, rows, dim), BF16),
        vmem((heads, dim, rows), BF16),
        vmem((heads, dim, rows), BF16),
        vmem((nodes, heads, dim, dim), BF16),
        vmem((heads, dim, rows), F32),
        vmem((heads, dim, dim), BF16),
    ]
    scratch += [vmem((heads, dim >> depth[bit], dim), BF16) for bit in range(1, bits)]
    scratch += [vmem((heads, dim, dim), BF16) for _ in range(bits)]
    scratch += [
        dma((len(moves), chunks)),
        dma((len(moves), chunks)),
        dma((2,)),
        dma((2,)),
        dma((3,)),
        dma((heads // group,)),
        dma((heads // group,)),
    ]
    anywhere = pl.BlockSpec(memory_space=pl.ANY)
    mixed = pl.pallas_call(
        functools.partial(kernel, sizes),
        in_specs=[anywhere] * 4,
        out_specs=pl.BlockSpec(memory_space=pltpu.VMEM),
        out_shape=vmem((rows, width), BF16),
        scratch_shapes=scratch,
        compiler_params=pltpu.CompilerParams(
            collective_id=0, has_side_effects=True, vmem_limit_bytes=56 * 2**20
        ),
        name="attend",
    )(projected, conv_weight, level_codes, out_gain.reshape(1, width))
    pieces = 8

    def deliver(source, target, sem):
        def piece(at):
            span = pl.ds(at * rows // pieces, rows // pieces)
            return pltpu.make_async_copy(source.at[span], target.at[span], sem.at[at])

        for at in range(pieces):
            piece(at).start()
        for at in range(pieces):
            piece(at).wait()

    return pl.pallas_call(
        deliver,
        in_specs=[pl.BlockSpec(memory_space=pltpu.VMEM)],
        out_specs=anywhere,
        out_shape=jax.ShapeDtypeStruct((rows, width), BF16),
        scratch_shapes=[dma((pieces,))],
        compiler_params=pltpu.CompilerParams(vmem_limit_bytes=2**20),
        name="deliver",
    )(mixed)


def solution(mesh):
    placed = (P(None, ("groups", "ctx"), None), P(), P(None, None, ("groups", "ctx")), P())
    return jax.shard_map(
        on_device, mesh=mesh, in_specs=placed, out_specs=P(("groups", "ctx"), None), check_vma=False
    )
```

```python
import functools

import jax
import jax.numpy as jnp
from jax import lax
from jax.experimental import pallas as pl
from jax.experimental.pallas import tpu as pltpu
from jax.sharding import PartitionSpec as P

PAD = 8
TILE = 128
MESH = pl.DeviceIdType.MESH
F32, BF16 = jnp.float32, jnp.bfloat16
BEHIND = 12
CHUNK = 2
INC = (2, 4, 4, 4, 2)


def spread(count, dim):
    bits = count.bit_length() - 1
    depth = [0] + [1] * (bits - 2) + [min(2, bits - 1)] if bits > 1 else [0]
    swaps = [("swap", bit, 0) for bit in range(bits)]
    shares = [("share", bit, at) for bit in range(bits) for at in reversed(range(depth[bit]))]
    return bits, depth, swaps + shares


def kernel(sizes, *refs):
    heads, dim, rows, taps, level_count, count, chunk, group = sizes
    bits, depth, moves = spread(count, dim)
    chunks = heads // chunk
    width = heads * dim
    tok_bits = rows.bit_length() - 1
    block = min(2 * TILE, rows)
    blocks = rows // block
    block_bits = blocks.bit_length() - 1
    top = TILE.bit_length() - 1
    strip = PAD.bit_length() - 1
    nodes = [(bit, at) for bit in range(block_bits) for at in range(0, blocks >> bit, 2)]

    projected, conv_weight, codes, gain, mixed = refs[:5]
    xs, taps_in, code_in, lam, gains, rim, held, outer = refs[5:13]
    keys, values_t, queries_t, inner, within, state = refs[13:19]
    accs = [state] + list(refs[19 : 19 + bits - 1])
    gots = refs[18 + bits : 18 + 2 * bits]
    send_sem, recv_sem, rim_send, rim_recv, small_sem, kv_sem, q_sem = refs[18 + 2 * bits :]

    part = lax.axis_index("groups")
    me = lax.axis_index("ctx")

    def region(level):
        start = 0
        for step in range(level):
            start = start + ((me >> step) & 1) * (dim >> (step + 1))
        return pl.ds(pl.multiple_of(start, dim >> level), dim >> level)

    def transfer(move, g):
        kind, bit, at = moves[move]
        which = pl.ds(g * chunk, chunk)
        if kind == "swap":
            source, target = accs[bit].at[which], gots[bit].at[which, region(depth[bit])]
            to = me ^ (1 << bit)
        else:
            source = target = gots[bit].at[which, region(at + 1)]
            to = me ^ (1 << at)
        return pltpu.make_async_remote_copy(
            src_ref=source,
            dst_ref=target,
            send_sem=send_sem.at[move, g],
            recv_sem=recv_sem.at[move, g],
            device_id=(part, to),
            device_id_type=MESH,
        )

    def small(index):
        pair = [(conv_weight, taps_in), (codes, code_in), (gain, gains)][index]
        return pltpu.make_async_copy(*pair, small_sem.at[index])

    def load(kind, g, sem):
        lanes = pl.ds(g * group * dim, group * dim)
        return pltpu.make_async_copy(projected.at[kind, :, lanes], xs.at[kind, :, lanes], sem)

    def load_kv(g):
        lanes = pl.ds(pl.multiple_of(g * group * dim, group * dim), group * dim)
        return pltpu.make_async_copy(
            projected.at[pl.ds(1, 2), :, lanes], xs.at[pl.ds(1, 2), :, lanes], kv_sem.at[g]
        )

    def load_q(g):
        lanes = pl.ds(pl.multiple_of(g * group * dim, group * dim), group * dim)
        return pltpu.make_async_copy(projected.at[0, :, lanes], xs.at[0, :, lanes], q_sem.at[g])

    def rim_copy(index):
        first = group * dim
        lanes = [pl.ds(0, first), pl.ds(first, width - first)][index]
        return pltpu.make_async_remote_copy(
            src_ref=projected.at[:, pl.ds(rows - PAD, PAD), lanes],
            dst_ref=rim.at[:, :, lanes],
            send_sem=rim_send.at[index],
            recv_sem=rim_recv.at[index],
            device_id=(part, me + 1),
            device_id_type=MESH,
        )

    for index in range(3):
        small(index).start()
    for g in range(heads // group):
        load_kv(g).start()
    for g in range(heads // group):
        load_q(g).start()

    barrier = pltpu.get_barrier_semaphore()
    for bit in range(bits):
        pl.semaphore_signal(barrier, inc=1, device_id=(part, me ^ (1 << bit)), device_id_type=MESH)
    odd = me & 1
    beside = me + 2 * odd - 1
    has_beside = (beside >= 0) & (beside < count)

    @pl.when(has_beside)
    def _():
        pl.semaphore_signal(barrier, inc=1, device_id=(part, beside), device_id_type=MESH)

    pl.semaphore_wait(barrier, bits + jnp.where(has_beside, 1, 0))

    @pl.when(me < count - 1)
    def _():
        rim_copy(0).start()
        rim_copy(1).start()

    @pl.when(me == 0)
    def _():
        rim[...] = jnp.zeros_like(rim)

    for index in range(3):
        small(index).wait()
    for level in range(level_count):
        scale = 0.125
        if level > tok_bits:
            scale = ((me >> (level - tok_bits - 1)) & 1).astype(F32) * 0.125
        for tile in range(rows // TILE):
            lanes = slice(tile * TILE, (tile + 1) * TILE)
            lam[level, tile] = code_in[level, :, lanes].astype(F32) * scale

    @pl.when(me > 0)
    def _():
        rim_copy(0).wait_recv()

    pieces = rows // TILE

    def convolve(kind, head, slot, piece):
        lanes = pl.ds(pl.multiple_of(head * dim, dim), dim)
        line = held.at[slot]
        start = piece * TILE
        if piece == 0:
            line[0:PAD, :] = rim[kind, :, lanes].astype(F32)
        own = xs[kind, start : start + TILE, lanes].astype(F32)
        line[PAD + start : PAD + start + TILE, :] = own
        total = taps_in[kind, taps - 1 : taps, lanes] * own
        for tap in range(taps - 1):
            first = PAD - taps + 1 + tap + start
            total = total + taps_in[kind, tap : tap + 1, lanes] * line[first : first + TILE, :]
        return total.astype(BF16)

    def states(head, slot):
        sums, per = [], block // TILE
        for at in range(blocks):
            key, value_t = [], []
            for piece in range(at * per, (at + 1) * per):
                span = slice(piece * TILE, (piece + 1) * TILE)
                key.append(convolve(1, head, 2 * slot, piece))
                keys[head, span, :] = key[-1]
                yield
                value_t.append(convolve(2, head, 2 * slot + 1, piece).T)
                values_t[head, :, span] = value_t[-1]
                yield
            sums.append(
                jnp.dot(
                    jnp.concatenate(value_t, 1),
                    jnp.concatenate(key, 0),
                    preferred_element_type=F32,
                )
            )
            yield
        for number, (bit, at) in enumerate(nodes):
            inner[number, head] = sum(sums[at << bit : (at + 1) << bit]).astype(BF16)
        state[head] = sum(sums).astype(BF16)

    strips = TILE // PAD
    lane8 = lax.broadcasted_iota(jnp.int32, (PAD, TILE), 1)
    row8 = lax.broadcasted_iota(jnp.int32, (PAD, TILE), 0)
    lane_strip = lax.broadcasted_iota(jnp.int32, (strips, TILE), 1) >> strip
    row_strip = lax.broadcasted_iota(jnp.int32, (strips, TILE), 0)

    def lam_row(level, head, span):
        tiles = range(span.start // TILE, span.stop // TILE)
        return jnp.concatenate([lam[level, tile, pl.ds(head, 1), :] for tile in tiles], 1)

    def diagonal(head, tile, slot):
        span = slice(tile * TILE, (tile + 1) * TILE)
        differ = lane_strip ^ row_strip
        wide = jnp.broadcast_to(lam_row(top, head, span), differ.shape)
        for level in range(top - 1, strip, -1):
            wide = jnp.where(differ < 2 ** (level - strip), lam_row(level, head, span), wide)
        outer[slot, :, span] = jnp.where(row_strip <= lane_strip, wide, 0.0)
        differ8 = (lane8 & (PAD - 1)) ^ row8
        near = jnp.broadcast_to(lam_row(strip, head, span), differ8.shape)
        for level in range(strip - 1, -1, -1):
            near = jnp.where(differ8 < 2**level, lam_row(level, head, span), near)
        near = jnp.where(row8 <= (lane8 & (PAD - 1)), near, 0.0)
        own = lane8 >> strip
        return jnp.concatenate(
            [jnp.where(own == number, near, outer[slot, number : number + 1, span]) for number in range(strips)], 0
        )

    def inside(head, slot):
        tiles = block // TILE
        query_t, scores = [], []
        for at in range(blocks):
            for piece in range(at * tiles, (at + 1) * tiles):
                span = slice(piece * TILE, (piece + 1) * TILE)
                query_t.append(convolve(0, head, 2 * chunk + slot, piece).T)
                queries_t[head, :, span] = query_t[-1]
                yield
            span = slice(at * block, (at + 1) * block)
            scores.append(
                jnp.dot(
                    keys[head, span, :],
                    jnp.concatenate(query_t[-tiles:], 1),
                    preferred_element_type=F32,
                )
            )
            yield
        for at in range(blocks):
            span = slice(at * block, (at + 1) * block)
            columns = []
            for tile in range(tiles):
                place = at * tiles + tile
                lanes = slice(tile * TILE, (tile + 1) * TILE)
                chosen = []
                for other in range(tiles):
                    score = scores[at][other * TILE : (other + 1) * TILE, lanes]
                    if other > tile:
                        chosen.append(jnp.zeros((TILE, TILE), BF16))
                        continue
                    if other == tile:
                        factor = diagonal(head, place, slot)
                    else:
                        level = top + (other ^ tile).bit_length()
                        factor = lam_row(level, head, slice(place * TILE, (place + 1) * TILE))
                    chosen.append((score * factor).astype(BF16))
                    yield
                columns.append(jnp.concatenate(chosen, 0))
            left = [values_t[head, :, span]]
            right = [jnp.concatenate(columns, 1)]
            for bit in range(block_bits):
                if at >> bit & 1:
                    node = nodes.index((bit, (at >> bit) - 1))
                    level = block.bit_length() + bit
                    query = jnp.concatenate(query_t[at * tiles : (at + 1) * tiles], 1)
                    scaled = query.astype(F32) * lam_row(level, head, span)
                    left.append(inner[node, head])
                    right.append(scaled.astype(BF16))
            within[head, :, span] = jnp.dot(
                jnp.concatenate(left, 1), jnp.concatenate(right, 0), preferred_element_type=F32
            )
            yield

    def mix(head, at):
        lanes = pl.ds(pl.multiple_of(head * dim, dim), dim)
        span = slice(at * block, (at + 1) * block)
        query_t = queries_t[head, :, span].astype(F32)
        right = [
            (query_t * lam_row(tok_bits + 1 + bit, head, span)).astype(BF16) for bit in range(bits)
        ]
        left = [gots[bit][head] for bit in range(bits)]
        yield
        total = within[head, :, span] + jnp.dot(
            jnp.concatenate(left, 1), jnp.concatenate(right, 0), preferred_element_type=F32
        )
        yield
        inverse = lax.rsqrt(jnp.mean(total * total, 0, keepdims=True) + 1e-06)
        flat = (total * inverse).T
        yield
        mixed[span, lanes] = (flat * gains[0:1, lanes]).astype(BF16)

    def together(streams):
        streams = list(streams)
        while streams:
            streams = [stream for stream in streams if next(stream, streams) is not streams]

    def states_of(g):
        return [states(g * chunk + index, index) for index in range(chunk)]

    def inside_of(g):
        return [inside(g * chunk + index, index) for index in range(chunk)]

    def mix_of(g):
        return [mix(g * chunk + index, at) for index in range(chunk) for at in range(blocks)]

    lag, at = {}, 0
    for bit in range(bits):
        at += INC[min(bit, 1)] if bit < bits - 1 else INC[2]
        lag[bit] = at
    for move in range(bits, len(moves)):
        _, bit, place = moves[move]
        if bit == bits - 1 and place:
            at += INC[3]
            lag[move] = at
    finish = at + INC[4]

    def handle(move, g):
        kind, bit, place = moves[move]
        transfer(move, g).wait_recv()
        if kind == "swap":
            if bit < bits - 1:
                which = pl.ds(g * chunk, chunk)
                size = dim >> depth[bit + 1]
                mine = region(depth[bit + 1])
                if depth[bit + 1] == depth[bit]:
                    old = accs[bit][which]
                else:
                    start = 0
                    for step in range(depth[bit], depth[bit + 1]):
                        start = start + ((me >> step) & 1) * (dim >> (step + 1))
                    old = accs[bit][which, pl.ds(pl.multiple_of(start, size), size), :]
                total = old.astype(F32) + gots[bit][which, mine, :].astype(F32)
                accs[bit + 1][which] = total.astype(BF16)
                transfer(bit + 1, g).start()
            if depth[bit]:
                transfer(moves.index(("share", bit, depth[bit] - 1)), g).start()
        else:
            transfer(moves.index(("share", bit, place - 1)), g).start()

    ordered = sorted(lag, key=lambda move: -lag[move])
    final = [move for move in range(len(moves)) if move not in lag]
    gate = group // chunk

    def fetch(g, load):
        @pl.when(lax.rem(g, gate) == 0)
        def _():
            load(g // gate).wait()

    def step(t, carry):
        for move in ordered:
            g = t - lag[move]

            @pl.when((g >= 0) & (g < chunks))
            def _(move=move, g=g):
                handle(move, g)

        @pl.when((t == 1) & (me > 0))
        def _():
            rim_copy(1).wait_recv()

        works = [(0, load_kv, states_of), (BEHIND, load_q, inside_of), (finish, None, mix_of)]
        ready = [(t >= late) & (t < late + chunks) for late, _, _ in works]
        for (late, load, _), here in zip(works, ready):
            if load:

                @pl.when(here)
                def _(late=late, load=load):
                    fetch(t - late, load)

        @pl.when(ready[2])
        def _():
            for move in final:
                transfer(move, t - finish).wait_recv()

        for some in range(1, 8):
            chosen = [some >> place & 1 == 1 for place in range(3)]
            lates = [late for (late, _, _), own in zip(works, chosen) if own]
            if max(lates) - min(lates) >= chunks:
                continue
            wanted = True
            for own, here in zip(chosen, ready):
                wanted = wanted & (here if own else jnp.logical_not(here))

            @pl.when(wanted)
            def _(chosen=chosen):
                streams = []
                for own, (late, _, work) in reversed(list(zip(chosen, works))):
                    if own:
                        streams += work(t - late)
                together(streams)

                if chosen[0]:
                    transfer(0, t).start()

        return carry

    lax.fori_loop(0, max(finish, BEHIND) + chunks, step, 0)

    def drain(g, carry):
        for move in range(len(moves)):
            transfer(move, g).wait_send()
        return carry

    lax.fori_loop(0, chunks, drain, 0)

    @pl.when(me < count - 1)
    def _():
        rim_copy(0).wait_send()
        rim_copy(1).wait_send()


def on_device(projected, conv_weight, level_codes, out_gain):
    kinds, rows, width = projected.shape
    taps = conv_weight.shape[1]
    level_count, heads = level_codes.shape[:2]
    dim = width // heads
    count = lax.axis_size("ctx")
    chunk, group = CHUNK, 4
    chunks = heads // chunk
    bits, depth, moves = spread(count, dim)
    block = min(2 * TILE, rows)
    nodes = max(1, rows // block - 1)
    sizes = (heads, dim, rows, taps, level_count, count, chunk, group)
    vmem, dma = pltpu.VMEM, pltpu.SemaphoreType.DMA
    scratch = [
        vmem((kinds, rows, width), BF16),
        vmem(conv_weight.shape, F32),
        vmem((level_count, heads, rows), jnp.int32),
        vmem((level_count, rows // TILE, heads, TILE), F32),
        vmem((1, width), F32),
        vmem((kinds, PAD, width), BF16),
        vmem((3 * chunk, PAD + rows, dim), F32),
        vmem((chunk, TILE // PAD, rows), F32),
        vmem((heads, rows, dim), BF16),
        vmem((heads, dim, rows), BF16),
        vmem((heads, dim, rows), BF16),
        vmem((nodes, heads, dim, dim), BF16),
        vmem((heads, dim, rows), F32),
        vmem((heads, dim, dim), BF16),
    ]
    scratch += [vmem((heads, dim >> depth[bit], dim), BF16) for bit in range(1, bits)]
    scratch += [vmem((heads, dim, dim), BF16) for _ in range(bits)]
    scratch += [
        dma((len(moves), chunks)),
        dma((len(moves), chunks)),
        dma((2,)),
        dma((2,)),
        dma((3,)),
        dma((heads // group,)),
        dma((heads // group,)),
    ]
    anywhere = pl.BlockSpec(memory_space=pl.ANY)
    mixed = pl.pallas_call(
        functools.partial(kernel, sizes),
        in_specs=[anywhere] * 4,
        out_specs=pl.BlockSpec(memory_space=pltpu.VMEM),
        out_shape=vmem((rows, width), BF16),
        scratch_shapes=scratch,
        compiler_params=pltpu.CompilerParams(
            collective_id=0, has_side_effects=True, vmem_limit_bytes=56 * 2**20
        ),
        name="attend",
    )(projected, conv_weight, level_codes, out_gain.reshape(1, width))
    pieces = 8

    def deliver(source, target, sem):
        def piece(at):
            span = pl.ds(at * rows // pieces, rows // pieces)
            return pltpu.make_async_copy(source.at[span], target.at[span], sem.at[at])

        for at in range(pieces):
            piece(at).start()
        for at in range(pieces):
            piece(at).wait()

    return pl.pallas_call(
        deliver,
        in_specs=[pl.BlockSpec(memory_space=pltpu.VMEM)],
        out_specs=anywhere,
        out_shape=jax.ShapeDtypeStruct((rows, width), BF16),
        scratch_shapes=[dma((pieces,))],
        compiler_params=pltpu.CompilerParams(vmem_limit_bytes=2**20),
        name="deliver",
    )(mixed)


def solution(mesh):
    placed = (P(None, ("groups", "ctx"), None), P(), P(None, None, ("groups", "ctx")), P())
    return jax.shard_map(
        on_device, mesh=mesh, in_specs=placed, out_specs=P(("groups", "ctx"), None), check_vma=False
    )
```

```python
import functools

import jax
import jax.numpy as jnp
from jax import lax
from jax.experimental import pallas as pl
from jax.experimental.pallas import tpu as pltpu
from jax.sharding import PartitionSpec as P

PAD = 8
TILE = 128
MESH = pl.DeviceIdType.MESH
F32, BF16 = jnp.float32, jnp.bfloat16
BEHIND = 12
TAIL = 4
CHUNK = 2
INC = (2, 4, 4, 0, 4)


def spread(count, dim):
    bits = count.bit_length() - 1
    depth = [0] + [1] * (bits - 2) + [min(2, bits - 1)] if bits > 1 else [0]
    swaps = [("swap", bit, 0) for bit in range(bits)]
    shares = [("share", bit, at) for bit in range(bits) for at in range(1, 1 << depth[bit])]
    return bits, depth, swaps + shares


def lam_of(lam, level, head, span):
    tiles = range(span.start // TILE, span.stop // TILE)
    return jnp.concatenate([lam[level, tile, pl.ds(head, 1), :] for tile in tiles], 1)


def mix(shape, refs, out, head, start, at):
    dim, block, base = shape
    within, queries_t, lam, gains = refs[:4]
    gots = refs[4:]
    span = slice(at * block, (at + 1) * block)
    query_t = queries_t[head, :, span].astype(F32)
    right = [
        (query_t * lam_of(lam, base + bit, head, span)).astype(BF16) for bit in range(len(gots))
    ]
    left = [got[head] for got in gots]
    yield
    total = within[head, :, span] + jnp.dot(
        jnp.concatenate(left, 1), jnp.concatenate(right, 0), preferred_element_type=F32
    )
    yield
    inverse = lax.rsqrt(jnp.mean(total * total, 0, keepdims=True) + 1e-06)
    flat = (total * inverse).T
    yield
    out[span, start] = (flat * gains[0:1, lanes_of(head, dim)]).astype(BF16)


def lanes_of(head, dim):
    start = head * dim
    return pl.ds(start if isinstance(head, int) else pl.multiple_of(start, dim), dim)


def together(streams):
    streams = list(streams)
    while streams:
        streams = [stream for stream in streams if next(stream, streams) is not streams]


def kernel(sizes, *refs):
    heads, dim, rows, taps, level_count, count, chunk, group, tail = sizes
    bits, depth, moves = spread(count, dim)
    chunks = heads // chunk
    width = heads * dim
    tok_bits = rows.bit_length() - 1
    block = min(2 * TILE, rows)
    blocks = rows // block
    block_bits = blocks.bit_length() - 1
    top = TILE.bit_length() - 1
    strip = PAD.bit_length() - 1
    nodes = [(bit, at) for bit in range(block_bits) for at in range(0, blocks >> bit, 2)]

    projected, conv_weight, codes, gain, mixed = refs[:5]
    within, queries_t, lam, gains = refs[5:9]
    gots = refs[9 : 9 + bits]
    refs = refs[9 + bits :]
    xs, taps_in, code_in, rim, held, outer, keys, values_t, inner, state = refs[:10]
    accs = [state] + list(refs[10 : 9 + bits])
    send_sem, recv_sem, rim_send, rim_recv, small_sem, kv_sem, q_sem = refs[9 + bits :]

    part = lax.axis_index("groups")
    me = lax.axis_index("ctx")

    def region(level):
        start = 0
        for step in range(level):
            start = start + ((me >> step) & 1) * (dim >> (step + 1))
        return pl.ds(pl.multiple_of(start, dim >> level), dim >> level)

    def transfer(move, g):
        kind, bit, at = moves[move]
        which = pl.ds(g * chunk, chunk)
        if kind == "swap":
            source, target = accs[bit].at[which], gots[bit].at[which, region(depth[bit])]
            to = me ^ (1 << bit)
        else:
            source = target = gots[bit].at[which, region(depth[bit])]
            to = me ^ at
        return pltpu.make_async_remote_copy(
            src_ref=source,
            dst_ref=target,
            send_sem=send_sem.at[move, g],
            recv_sem=recv_sem.at[move, g],
            device_id=(part, to),
            device_id_type=MESH,
        )

    def small(index):
        pair = [(conv_weight, taps_in), (codes, code_in), (gain, gains)][index]
        return pltpu.make_async_copy(*pair, small_sem.at[index])

    def load(kind, g, sem):
        lanes = pl.ds(g * group * dim, group * dim)
        return pltpu.make_async_copy(projected.at[kind, :, lanes], xs.at[kind, :, lanes], sem)

    def load_kv(g):
        lanes = pl.ds(pl.multiple_of(g * group * dim, group * dim), group * dim)
        return pltpu.make_async_copy(
            projected.at[pl.ds(1, 2), :, lanes], xs.at[pl.ds(1, 2), :, lanes], kv_sem.at[g]
        )

    def load_q(g):
        lanes = pl.ds(pl.multiple_of(g * group * dim, group * dim), group * dim)
        return pltpu.make_async_copy(projected.at[0, :, lanes], xs.at[0, :, lanes], q_sem.at[g])

    def rim_copy(index):
        first = group * dim
        lanes = [pl.ds(0, first), pl.ds(first, width - first)][index]
        return pltpu.make_async_remote_copy(
            src_ref=projected.at[:, pl.ds(rows - PAD, PAD), lanes],
            dst_ref=rim.at[:, :, lanes],
            send_sem=rim_send.at[index],
            recv_sem=rim_recv.at[index],
            device_id=(part, me + 1),
            device_id_type=MESH,
        )

    for index in range(3):
        small(index).start()
    for g in range(heads // group):
        load_kv(g).start()
    for g in range(heads // group):
        load_q(g).start()

    barrier = pltpu.get_barrier_semaphore()
    for bit in range(bits):
        pl.semaphore_signal(barrier, inc=1, device_id=(part, me ^ (1 << bit)), device_id_type=MESH)
    odd = me & 1
    beside = me + 2 * odd - 1
    has_beside = (beside >= 0) & (beside < count)

    @pl.when(has_beside)
    def _():
        pl.semaphore_signal(barrier, inc=1, device_id=(part, beside), device_id_type=MESH)

    pl.semaphore_wait(barrier, bits + jnp.where(has_beside, 1, 0))

    @pl.when(me < count - 1)
    def _():
        rim_copy(0).start()
        rim_copy(1).start()

    @pl.when(me == 0)
    def _():
        rim[...] = jnp.zeros_like(rim)

    for index in range(3):
        small(index).wait()
    for level in range(level_count):
        scale = 0.125
        if level > tok_bits:
            scale = ((me >> (level - tok_bits - 1)) & 1).astype(F32) * 0.125
        for tile in range(rows // TILE):
            lanes = slice(tile * TILE, (tile + 1) * TILE)
            lam[level, tile] = code_in[level, :, lanes].astype(F32) * scale

    @pl.when(me > 0)
    def _():
        rim_copy(0).wait_recv()

    pieces = rows // TILE

    def convolve(kind, head, slot, piece):
        lanes = pl.ds(pl.multiple_of(head * dim, dim), dim)
        line = held.at[slot]
        start = piece * TILE
        if piece == 0:
            line[0:PAD, :] = rim[kind, :, lanes].astype(F32)
        own = xs[kind, start : start + TILE, lanes].astype(F32)
        line[PAD + start : PAD + start + TILE, :] = own
        total = taps_in[kind, taps - 1 : taps, lanes] * own
        for tap in range(taps - 1):
            first = PAD - taps + 1 + tap + start
            total = total + taps_in[kind, tap : tap + 1, lanes] * line[first : first + TILE, :]
        return total.astype(BF16)

    def states(head, slot):
        sums, per = [], block // TILE
        for at in range(blocks):
            key, value_t = [], []
            for piece in range(at * per, (at + 1) * per):
                span = slice(piece * TILE, (piece + 1) * TILE)
                key.append(convolve(1, head, 2 * slot, piece))
                keys[head, span, :] = key[-1]
                yield
                value_t.append(convolve(2, head, 2 * slot + 1, piece).T)
                values_t[head, :, span] = value_t[-1]
                yield
            sums.append(
                jnp.dot(
                    jnp.concatenate(value_t, 1),
                    jnp.concatenate(key, 0),
                    preferred_element_type=F32,
                )
            )
            yield
        for number, (bit, at) in enumerate(nodes):
            inner[number, head] = sum(sums[at << bit : (at + 1) << bit]).astype(BF16)
        state[head] = sum(sums).astype(BF16)

    strips = TILE // PAD
    lane8 = lax.broadcasted_iota(jnp.int32, (PAD, TILE), 1)
    row8 = lax.broadcasted_iota(jnp.int32, (PAD, TILE), 0)
    lane_strip = lax.broadcasted_iota(jnp.int32, (strips, TILE), 1) >> strip
    row_strip = lax.broadcasted_iota(jnp.int32, (strips, TILE), 0)

    def lam_row(level, head, span):
        tiles = range(span.start // TILE, span.stop // TILE)
        return jnp.concatenate([lam[level, tile, pl.ds(head, 1), :] for tile in tiles], 1)

    def diagonal(head, tile, slot):
        span = slice(tile * TILE, (tile + 1) * TILE)
        differ = lane_strip ^ row_strip
        wide = jnp.broadcast_to(lam_row(top, head, span), differ.shape)
        for level in range(top - 1, strip, -1):
            wide = jnp.where(differ < 2 ** (level - strip), lam_row(level, head, span), wide)
        outer[slot, :, span] = jnp.where(row_strip <= lane_strip, wide, 0.0)
        differ8 = (lane8 & (PAD - 1)) ^ row8
        near = jnp.broadcast_to(lam_row(strip, head, span), differ8.shape)
        for level in range(strip - 1, -1, -1):
            near = jnp.where(differ8 < 2**level, lam_row(level, head, span), near)
        near = jnp.where(row8 <= (lane8 & (PAD - 1)), near, 0.0)
        own = lane8 >> strip
        return jnp.concatenate(
            [jnp.where(own == number, near, outer[slot, number : number + 1, span]) for number in range(strips)], 0
        )

    def inside(head, slot):
        tiles = block // TILE
        query_t, scores = [], []
        for at in range(blocks):
            for piece in range(at * tiles, (at + 1) * tiles):
                span = slice(piece * TILE, (piece + 1) * TILE)
                query_t.append(convolve(0, head, 2 * chunk + slot, piece).T)
                queries_t[head, :, span] = query_t[-1]
                yield
            span = slice(at * block, (at + 1) * block)
            scores.append(
                jnp.dot(
                    keys[head, span, :],
                    jnp.concatenate(query_t[-tiles:], 1),
                    preferred_element_type=F32,
                )
            )
            yield
        for at in range(blocks):
            span = slice(at * block, (at + 1) * block)
            columns = []
            for tile in range(tiles):
                place = at * tiles + tile
                lanes = slice(tile * TILE, (tile + 1) * TILE)
                chosen = []
                for other in range(tiles):
                    score = scores[at][other * TILE : (other + 1) * TILE, lanes]
                    if other > tile:
                        chosen.append(jnp.zeros((TILE, TILE), BF16))
                        continue
                    if other == tile:
                        factor = diagonal(head, place, slot)
                    else:
                        level = top + (other ^ tile).bit_length()
                        factor = lam_row(level, head, slice(place * TILE, (place + 1) * TILE))
                    chosen.append((score * factor).astype(BF16))
                    yield
                columns.append(jnp.concatenate(chosen, 0))
            left = [values_t[head, :, span]]
            right = [jnp.concatenate(columns, 1)]
            for bit in range(block_bits):
                if at >> bit & 1:
                    node = nodes.index((bit, (at >> bit) - 1))
                    level = block.bit_length() + bit
                    query = jnp.concatenate(query_t[at * tiles : (at + 1) * tiles], 1)
                    scaled = query.astype(F32) * lam_row(level, head, span)
                    left.append(inner[node, head])
                    right.append(scaled.astype(BF16))
            within[head, :, span] = jnp.dot(
                jnp.concatenate(left, 1), jnp.concatenate(right, 0), preferred_element_type=F32
            )
            yield

    def states_of(g):
        return [states(g * chunk + index, index) for index in range(chunk)]

    def inside_of(g):
        return [inside(g * chunk + index, index) for index in range(chunk)]

    def mix_of(g):
        shape = (dim, block, tok_bits + 1)
        given = [within, queries_t, lam, gains] + list(gots)
        return [
            mix(shape, given, mixed, g * chunk + index, lanes_of(g * chunk + index, dim), at)
            for index in range(chunk)
            for at in range(blocks)
        ]

    lag, at = {}, 0
    for bit in range(bits):
        at += INC[min(bit, 1)] if bit < bits - 1 else INC[2]
        lag[bit] = at
    finish = at + INC[4]

    def handle(move, g):
        kind, bit, place = moves[move]
        transfer(move, g).wait_recv()
        if kind == "swap":
            if bit < bits - 1:
                which = pl.ds(g * chunk, chunk)
                size = dim >> depth[bit + 1]
                mine = region(depth[bit + 1])
                if depth[bit + 1] == depth[bit]:
                    old = accs[bit][which]
                else:
                    start = 0
                    for step in range(depth[bit], depth[bit + 1]):
                        start = start + ((me >> step) & 1) * (dim >> (step + 1))
                    old = accs[bit][which, pl.ds(pl.multiple_of(start, size), size), :]
                total = old.astype(F32) + gots[bit][which, mine, :].astype(F32)
                accs[bit + 1][which] = total.astype(BF16)
                transfer(bit + 1, g).start()
            for share in range(1, 1 << depth[bit]):
                transfer(moves.index(("share", bit, share)), g).start()

    ordered = sorted(lag, key=lambda move: lag[move])
    final = [move for move in range(len(moves)) if move not in lag]
    gate = group // chunk

    def fetch(g, load):
        @pl.when(lax.rem(g, gate) == 0)
        def _():
            load(g // gate).wait()

    def step(t, carry):
        for move in ordered:
            g = t - lag[move]

            @pl.when((g >= 0) & (g < chunks))
            def _(move=move, g=g):
                handle(move, g)

        @pl.when((t == 1) & (me > 0))
        def _():
            rim_copy(1).wait_recv()

        counts = [chunks, chunks, chunks - tail]
        works = [(0, load_kv, states_of), (BEHIND, load_q, inside_of), (finish, None, mix_of)]
        ready = [(t >= late) & (t < late + many) for (late, _, _), many in zip(works, counts)]
        for (late, load, _), here in zip(works, ready):
            if load:

                @pl.when(here)
                def _(late=late, load=load):
                    fetch(t - late, load)

        @pl.when(ready[2])
        def _():
            for move in final:
                transfer(move, t - finish).wait_recv()

        for some in range(1, 8):
            chosen = [some >> place & 1 == 1 for place in range(3)]
            lates = [late for (late, _, _), own in zip(works, chosen) if own]
            if max(lates) - min(lates) >= chunks:
                continue
            wanted = True
            for own, here in zip(chosen, ready):
                wanted = wanted & (here if own else jnp.logical_not(here))

            @pl.when(wanted)
            def _(chosen=chosen):
                streams = []
                for own, (late, _, work) in reversed(list(zip(chosen, works))):
                    if own:
                        streams += work(t - late)
                together(streams)

                if chosen[0]:
                    transfer(0, t).start()

        return carry

    last = max(max(lag.values()) + chunks, BEHIND + chunks, finish + chunks - tail)
    lax.fori_loop(0, last, step, 0)

    for g in range(chunks - tail, chunks):
        for move in final:
            transfer(move, g).wait_recv()

    def drain(g, carry):
        for move in range(len(moves)):
            transfer(move, g).wait_send()
        return carry

    lax.fori_loop(0, chunks, drain, 0)

    @pl.when(me < count - 1)
    def _():
        rim_copy(0).wait_send()
        rim_copy(1).wait_send()


def on_device(projected, conv_weight, level_codes, out_gain):
    kinds, rows, width = projected.shape
    taps = conv_weight.shape[1]
    level_count, heads = level_codes.shape[:2]
    dim = width // heads
    count = lax.axis_size("ctx")
    chunk, group, tail = CHUNK, 4, TAIL
    chunks = heads // chunk
    bits, depth, moves = spread(count, dim)
    block = min(2 * TILE, rows)
    nodes = max(1, rows // block - 1)
    sizes = (heads, dim, rows, taps, level_count, count, chunk, group, tail)
    vmem, dma = pltpu.VMEM, pltpu.SemaphoreType.DMA
    ahead = (chunks - tail) * chunk
    results = [
        vmem((rows, ahead * dim), BF16),
        vmem((heads, dim, rows), F32),
        vmem((heads, dim, rows), BF16),
        vmem((level_count, rows // TILE, heads, TILE), F32),
        vmem((1, width), F32),
    ] + [vmem((heads, dim, dim), BF16) for _ in range(bits)]
    scratch = [
        vmem((kinds, rows, width), BF16),
        vmem(conv_weight.shape, F32),
        vmem((level_count, heads, rows), jnp.int32),
        vmem((kinds, PAD, width), BF16),
        vmem((3 * chunk, PAD + rows, dim), F32),
        vmem((chunk, TILE // PAD, rows), F32),
        vmem((heads, rows, dim), BF16),
        vmem((heads, dim, rows), BF16),
        vmem((nodes, heads, dim, dim), BF16),
        vmem((heads, dim, dim), BF16),
    ]
    scratch += [vmem((heads, dim >> depth[bit], dim), BF16) for bit in range(1, bits)]
    scratch += [
        dma((len(moves), chunks)),
        dma((len(moves), chunks)),
        dma((2,)),
        dma((2,)),
        dma((3,)),
        dma((heads // group,)),
        dma((heads // group,)),
    ]
    anywhere = pl.BlockSpec(memory_space=pl.ANY)
    inside_vmem = pl.BlockSpec(memory_space=pltpu.VMEM)
    done = pl.pallas_call(
        functools.partial(kernel, sizes),
        in_specs=[pl.BlockSpec(memory_space=pltpu.HBM)] * 4,
        out_specs=[inside_vmem] * len(results),
        out_shape=results,
        scratch_shapes=scratch,
        compiler_params=pltpu.CompilerParams(
            collective_id=0, has_side_effects=True, vmem_limit_bytes=34 * 2**20
        ),
        name="attend",
    )(projected, conv_weight, level_codes, out_gain.reshape(1, width))
    tok_bits = rows.bit_length() - 1
    pieces = ahead * dim // (group * dim)

    def deliver(*refs):
        mixed, given = refs[0], refs[1 : 5 + bits]
        target, fresh, sem = refs[5 + bits :]

        def piece(at):
            lanes = pl.ds(at * group * dim, group * dim)
            return pltpu.make_async_copy(mixed.at[:, lanes], target.at[:, lanes], sem.at[at])

        def rest(at):
            lanes = pl.ds(at * chunk * dim, chunk * dim)
            lies = pl.ds((ahead + at * chunk) * dim, chunk * dim)
            return pltpu.make_async_copy(fresh.at[:, lanes], target.at[:, lies], sem.at[pieces + at])

        for at in range(pieces):
            piece(at).start()
        for at in range(tail):
            heads_here = range(ahead + at * chunk, ahead + (at + 1) * chunk)
            together(
                mix((dim, block, tok_bits + 1), given, fresh, head, lanes_of(head - ahead, dim), part)
                for head in heads_here
                for part in range(rows // block)
            )
            rest(at).start()
        for at in range(pieces):
            piece(at).wait()
        for at in range(tail):
            rest(at).wait()

    return pl.pallas_call(
        deliver,
        in_specs=[inside_vmem] * len(results),
        out_specs=anywhere,
        out_shape=jax.ShapeDtypeStruct((rows, width), BF16),
        scratch_shapes=[vmem((rows, max(1, tail * chunk) * dim), BF16), dma((pieces + tail,))],
        compiler_params=pltpu.CompilerParams(vmem_limit_bytes=4 * 2**20),
        name="deliver",
    )(*done)


def solution(mesh):
    placed = (P(None, ("groups", "ctx"), None), P(), P(None, None, ("groups", "ctx")), P())
    return jax.shard_map(
        on_device, mesh=mesh, in_specs=placed, out_specs=P(("groups", "ctx"), None), check_vma=False
    )
```

```python
import functools

import jax
import jax.numpy as jnp
from jax import lax
from jax.experimental import pallas as pl
from jax.experimental.pallas import tpu as pltpu
from jax.sharding import PartitionSpec as P

PAD = 8
TILE = 128
MESH = pl.DeviceIdType.MESH
F32, BF16 = jnp.float32, jnp.bfloat16
BEHIND = 12
TAIL = 4
CHUNK = 2
INC = (2, 4, 4, 0, 4)


def spread(count, dim):
    bits = count.bit_length() - 1
    depth = [0] + [1] * (bits - 2) + [min(2, bits - 1)] if bits > 1 else [0]
    swaps = [("swap", bit, 0) for bit in range(bits)]
    shares = [("share", bit, at) for bit in range(bits) for at in range(1, 1 << depth[bit])]
    return bits, depth, swaps + shares


def lam_of(lam, level, head, span):
    tiles = range(span.start // TILE, span.stop // TILE)
    return jnp.concatenate([lam[level, tile, pl.ds(head, 1), :] for tile in tiles], 1)


def mix(shape, refs, out, head, start, at):
    dim, block, base = shape
    within, queries_t, lam, gains = refs[:4]
    gots = refs[4:]
    span = slice(at * block, (at + 1) * block)
    query_t = queries_t[head, :, span]
    right = [
        query_t * lam_of(lam, base + bit, head, span).astype(BF16) for bit in range(len(gots))
    ]
    left = [got[head] for got in gots]
    yield
    total = within[head, :, span] + jnp.dot(
        jnp.concatenate(left, 1), jnp.concatenate(right, 0), preferred_element_type=F32
    )
    yield
    inverse = lax.rsqrt(jnp.mean(total * total, 0, keepdims=True) + 1e-06)
    flat = (total * inverse).T
    yield
    out[span, start] = (flat * gains[0:1, lanes_of(head, dim)]).astype(BF16)


def lanes_of(head, dim):
    start = head * dim
    return pl.ds(start if isinstance(head, int) else pl.multiple_of(start, dim), dim)


def together(streams):
    streams = list(streams)
    while streams:
        streams = [stream for stream in streams if next(stream, streams) is not streams]


def kernel(sizes, *refs):
    heads, dim, rows, taps, level_count, count, chunk, group, tail = sizes
    bits, depth, moves = spread(count, dim)
    chunks = heads // chunk
    width = heads * dim
    tok_bits = rows.bit_length() - 1
    block = min(2 * TILE, rows)
    blocks = rows // block
    block_bits = blocks.bit_length() - 1
    top = TILE.bit_length() - 1
    strip = PAD.bit_length() - 1
    nodes = [(bit, at) for bit in range(block_bits) for at in range(0, blocks >> bit, 2)]

    projected, conv_weight, codes, gain, mixed = refs[:5]
    within, queries_t, lam, gains = refs[5:9]
    gots = refs[9 : 9 + bits]
    refs = refs[9 + bits :]
    xs, taps_in, code_in, rim, held, outer, keys, values_t, inner, state = refs[:10]
    accs = [state] + list(refs[10 : 9 + bits])
    send_sem, recv_sem, rim_send, rim_recv, small_sem, kv_sem, q_sem = refs[9 + bits :]

    part = lax.axis_index("groups")
    me = lax.axis_index("ctx")

    def region(level):
        start = 0
        for step in range(level):
            start = start + ((me >> step) & 1) * (dim >> (step + 1))
        return pl.ds(pl.multiple_of(start, dim >> level), dim >> level)

    def transfer(move, g):
        kind, bit, at = moves[move]
        which = pl.ds(g * chunk, chunk)
        if kind == "swap":
            source, target = accs[bit].at[which], gots[bit].at[which, region(depth[bit])]
            to = me ^ (1 << bit)
        else:
            source = target = gots[bit].at[which, region(depth[bit])]
            to = me ^ at
        return pltpu.make_async_remote_copy(
            src_ref=source,
            dst_ref=target,
            send_sem=send_sem.at[move, g],
            recv_sem=recv_sem.at[move, g],
            device_id=(part, to),
            device_id_type=MESH,
        )

    def small(index):
        pair = [(conv_weight, taps_in), (codes, code_in), (gain, gains)][index]
        return pltpu.make_async_copy(*pair, small_sem.at[index])

    def load(kind, g, sem):
        lanes = pl.ds(g * group * dim, group * dim)
        return pltpu.make_async_copy(projected.at[kind, :, lanes], xs.at[kind, :, lanes], sem)

    def load_kv(g):
        lanes = pl.ds(pl.multiple_of(g * group * dim, group * dim), group * dim)
        return pltpu.make_async_copy(
            projected.at[pl.ds(1, 2), :, lanes], xs.at[pl.ds(1, 2), :, lanes], kv_sem.at[g]
        )

    def load_q(g):
        lanes = pl.ds(pl.multiple_of(g * group * dim, group * dim), group * dim)
        return pltpu.make_async_copy(projected.at[0, :, lanes], xs.at[0, :, lanes], q_sem.at[g])

    def rim_copy(index):
        first = group * dim
        lanes = [pl.ds(0, first), pl.ds(first, width - first)][index]
        return pltpu.make_async_remote_copy(
            src_ref=projected.at[:, pl.ds(rows - PAD, PAD), lanes],
            dst_ref=rim.at[:, :, lanes],
            send_sem=rim_send.at[index],
            recv_sem=rim_recv.at[index],
            device_id=(part, me + 1),
            device_id_type=MESH,
        )

    for index in range(3):
        small(index).start()
    for g in range(heads // group):
        load_kv(g).start()
    for g in range(heads // group):
        load_q(g).start()

    barrier = pltpu.get_barrier_semaphore()
    for bit in range(bits):
        pl.semaphore_signal(barrier, inc=1, device_id=(part, me ^ (1 << bit)), device_id_type=MESH)
    odd = me & 1
    beside = me + 2 * odd - 1
    has_beside = (beside >= 0) & (beside < count)

    @pl.when(has_beside)
    def _():
        pl.semaphore_signal(barrier, inc=1, device_id=(part, beside), device_id_type=MESH)

    pl.semaphore_wait(barrier, bits + jnp.where(has_beside, 1, 0))

    @pl.when(me < count - 1)
    def _():
        rim_copy(0).start()
        rim_copy(1).start()

    @pl.when(me == 0)
    def _():
        rim[...] = jnp.zeros_like(rim)

    for index in range(3):
        small(index).wait()
    for level in range(level_count):
        scale = 0.125
        if level > tok_bits:
            scale = ((me >> (level - tok_bits - 1)) & 1).astype(F32) * 0.125
        for tile in range(rows // TILE):
            lanes = slice(tile * TILE, (tile + 1) * TILE)
            lam[level, tile] = code_in[level, :, lanes].astype(F32) * scale

    @pl.when(me > 0)
    def _():
        rim_copy(0).wait_recv()

    pieces = rows // TILE

    def convolve(kind, head, slot, piece):
        lanes = pl.ds(pl.multiple_of(head * dim, dim), dim)
        line = held.at[slot]
        start = piece * TILE
        if piece == 0:
            line[0:PAD, :] = rim[kind, :, lanes].astype(F32)
        own = xs[kind, start : start + TILE, lanes].astype(F32)
        line[PAD + start : PAD + start + TILE, :] = own
        total = taps_in[kind, taps - 1 : taps, lanes] * own
        for tap in range(taps - 1):
            first = PAD - taps + 1 + tap + start
            total = total + taps_in[kind, tap : tap + 1, lanes] * line[first : first + TILE, :]
        return total.astype(BF16)

    def states(head, slot):
        sums, per = [], block // TILE
        for at in range(blocks):
            key, value_t = [], []
            for piece in range(at * per, (at + 1) * per):
                span = slice(piece * TILE, (piece + 1) * TILE)
                key.append(convolve(1, head, 2 * slot, piece))
                keys[head, span, :] = key[-1]
                yield
                value_t.append(convolve(2, head, 2 * slot + 1, piece).T)
                values_t[head, :, span] = value_t[-1]
                yield
            sums.append(
                jnp.dot(
                    jnp.concatenate(value_t, 1),
                    jnp.concatenate(key, 0),
                    preferred_element_type=F32,
                )
            )
            yield
        for number, (bit, at) in enumerate(nodes):
            inner[number, head] = sum(sums[at << bit : (at + 1) << bit]).astype(BF16)
        state[head] = sum(sums).astype(BF16)

    strips = TILE // PAD
    lane8 = lax.broadcasted_iota(jnp.int32, (PAD, TILE), 1)
    row8 = lax.broadcasted_iota(jnp.int32, (PAD, TILE), 0)
    lane_strip = lax.broadcasted_iota(jnp.int32, (strips, TILE), 1) >> strip
    row_strip = lax.broadcasted_iota(jnp.int32, (strips, TILE), 0)

    def lam_row(level, head, span):
        tiles = range(span.start // TILE, span.stop // TILE)
        return jnp.concatenate([lam[level, tile, pl.ds(head, 1), :] for tile in tiles], 1)

    def diagonal(head, tile, slot):
        span = slice(tile * TILE, (tile + 1) * TILE)
        differ = lane_strip ^ row_strip
        wide = jnp.broadcast_to(lam_row(top, head, span), differ.shape)
        for level in range(top - 1, strip, -1):
            wide = jnp.where(differ < 2 ** (level - strip), lam_row(level, head, span), wide)
        outer[slot, :, span] = jnp.where(row_strip <= lane_strip, wide, 0.0)
        differ8 = (lane8 & (PAD - 1)) ^ row8
        near = jnp.broadcast_to(lam_row(strip, head, span), differ8.shape)
        for level in range(strip - 1, -1, -1):
            near = jnp.where(differ8 < 2**level, lam_row(level, head, span), near)
        near = jnp.where(row8 <= (lane8 & (PAD - 1)), near, 0.0)
        own = lane8 >> strip
        return jnp.concatenate(
            [jnp.where(own == number, near, outer[slot, number : number + 1, span]) for number in range(strips)], 0
        )

    def inside(head, slot):
        tiles = block // TILE
        query_t, scores = [], []
        for at in range(blocks):
            for piece in range(at * tiles, (at + 1) * tiles):
                span = slice(piece * TILE, (piece + 1) * TILE)
                query_t.append(convolve(0, head, 2 * chunk + slot, piece).T)
                queries_t[head, :, span] = query_t[-1]
                yield
            span = slice(at * block, (at + 1) * block)
            scores.append(
                jnp.dot(
                    keys[head, span, :],
                    jnp.concatenate(query_t[-tiles:], 1),
                    preferred_element_type=F32,
                )
            )
            yield
        for at in range(blocks):
            span = slice(at * block, (at + 1) * block)
            columns = []
            for tile in range(tiles):
                place = at * tiles + tile
                lanes = slice(tile * TILE, (tile + 1) * TILE)
                chosen = []
                for other in range(tiles):
                    score = scores[at][other * TILE : (other + 1) * TILE, lanes]
                    if other > tile:
                        chosen.append(jnp.zeros((TILE, TILE), BF16))
                        continue
                    if other == tile:
                        factor = diagonal(head, place, slot)
                    else:
                        level = top + (other ^ tile).bit_length()
                        factor = lam_row(level, head, slice(place * TILE, (place + 1) * TILE))
                    chosen.append((score * factor).astype(BF16))
                    yield
                columns.append(jnp.concatenate(chosen, 0))
            left = [values_t[head, :, span]]
            right = [jnp.concatenate(columns, 1)]
            for bit in range(block_bits):
                if at >> bit & 1:
                    node = nodes.index((bit, (at >> bit) - 1))
                    level = block.bit_length() + bit
                    query = jnp.concatenate(query_t[at * tiles : (at + 1) * tiles], 1)
                    scaled = query.astype(F32) * lam_row(level, head, span)
                    left.append(inner[node, head])
                    right.append(scaled.astype(BF16))
            within[head, :, span] = jnp.dot(
                jnp.concatenate(left, 1), jnp.concatenate(right, 0), preferred_element_type=F32
            )
            yield

    def states_of(g):
        return [states(g * chunk + index, index) for index in range(chunk)]

    def inside_of(g):
        return [inside(g * chunk + index, index) for index in range(chunk)]

    def mix_of(g):
        shape = (dim, block, tok_bits + 1)
        given = [within, queries_t, lam, gains] + list(gots)
        return [
            mix(shape, given, mixed, g * chunk + index, lanes_of(g * chunk + index, dim), at)
            for index in range(chunk)
            for at in range(blocks)
        ]

    lag, at = {}, 0
    for bit in range(bits):
        at += INC[min(bit, 1)] if bit < bits - 1 else INC[2]
        lag[bit] = at
    finish = at + INC[4]

    def handle(move, g):
        kind, bit, place = moves[move]
        transfer(move, g).wait_recv()
        if kind == "swap":
            if bit < bits - 1:
                which = pl.ds(g * chunk, chunk)
                size = dim >> depth[bit + 1]
                mine = region(depth[bit + 1])
                if depth[bit + 1] == depth[bit]:
                    old = accs[bit][which]
                else:
                    start = 0
                    for step in range(depth[bit], depth[bit + 1]):
                        start = start + ((me >> step) & 1) * (dim >> (step + 1))
                    old = accs[bit][which, pl.ds(pl.multiple_of(start, size), size), :]
                total = old.astype(F32) + gots[bit][which, mine, :].astype(F32)
                accs[bit + 1][which] = total.astype(BF16)
                transfer(bit + 1, g).start()
            for share in range(1, 1 << depth[bit]):
                transfer(moves.index(("share", bit, share)), g).start()

    ordered = sorted(lag, key=lambda move: lag[move])
    final = [move for move in range(len(moves)) if move not in lag]
    gate = group // chunk

    def fetch(g, load):
        @pl.when(lax.rem(g, gate) == 0)
        def _():
            load(g // gate).wait()

    def step(t, carry):
        for move in ordered:
            g = t - lag[move]

            @pl.when((g >= 0) & (g < chunks))
            def _(move=move, g=g):
                handle(move, g)

        @pl.when((t == 1) & (me > 0))
        def _():
            rim_copy(1).wait_recv()

        counts = [chunks, chunks, chunks - tail]
        works = [(0, load_kv, states_of), (BEHIND, load_q, inside_of), (finish, None, mix_of)]
        ready = [(t >= late) & (t < late + many) for (late, _, _), many in zip(works, counts)]
        for (late, load, _), here in zip(works, ready):
            if load:

                @pl.when(here)
                def _(late=late, load=load):
                    fetch(t - late, load)

        @pl.when(ready[2])
        def _():
            for move in final:
                transfer(move, t - finish).wait_recv()

        for some in range(1, 8):
            chosen = [some >> place & 1 == 1 for place in range(3)]
            lates = [late for (late, _, _), own in zip(works, chosen) if own]
            if max(lates) - min(lates) >= chunks:
                continue
            wanted = True
            for own, here in zip(chosen, ready):
                wanted = wanted & (here if own else jnp.logical_not(here))

            @pl.when(wanted)
            def _(chosen=chosen):
                streams = []
                for own, (late, _, work) in reversed(list(zip(chosen, works))):
                    if own:
                        streams += work(t - late)
                together(streams)

                if chosen[0]:
                    transfer(0, t).start()

        return carry

    last = max(max(lag.values()) + chunks, BEHIND + chunks, finish + chunks - tail)
    lax.fori_loop(0, last, step, 0)

    for g in range(chunks - tail, chunks):
        for move in final:
            transfer(move, g).wait_recv()

    def drain(g, carry):
        for move in range(len(moves)):
            transfer(move, g).wait_send()
        return carry

    lax.fori_loop(0, chunks, drain, 0)

    @pl.when(me < count - 1)
    def _():
        rim_copy(0).wait_send()
        rim_copy(1).wait_send()


def on_device(projected, conv_weight, level_codes, out_gain):
    kinds, rows, width = projected.shape
    taps = conv_weight.shape[1]
    level_count, heads = level_codes.shape[:2]
    dim = width // heads
    count = lax.axis_size("ctx")
    chunk, group, tail = CHUNK, 4, TAIL
    chunks = heads // chunk
    bits, depth, moves = spread(count, dim)
    block = min(2 * TILE, rows)
    nodes = max(1, rows // block - 1)
    sizes = (heads, dim, rows, taps, level_count, count, chunk, group, tail)
    vmem, dma = pltpu.VMEM, pltpu.SemaphoreType.DMA
    ahead = (chunks - tail) * chunk
    results = [
        vmem((rows, ahead * dim), BF16),
        vmem((heads, dim, rows), F32),
        vmem((heads, dim, rows), BF16),
        vmem((level_count, rows // TILE, heads, TILE), F32),
        vmem((1, width), F32),
    ] + [vmem((heads, dim, dim), BF16) for _ in range(bits)]
    scratch = [
        vmem((kinds, rows, width), BF16),
        vmem(conv_weight.shape, F32),
        vmem((level_count, heads, rows), jnp.int32),
        vmem((kinds, PAD, width), BF16),
        vmem((3 * chunk, PAD + rows, dim), F32),
        vmem((chunk, TILE // PAD, rows), F32),
        vmem((heads, rows, dim), BF16),
        vmem((heads, dim, rows), BF16),
        vmem((nodes, heads, dim, dim), BF16),
        vmem((heads, dim, dim), BF16),
    ]
    scratch += [vmem((heads, dim >> depth[bit], dim), BF16) for bit in range(1, bits)]
    scratch += [
        dma((len(moves), chunks)),
        dma((len(moves), chunks)),
        dma((2,)),
        dma((2,)),
        dma((3,)),
        dma((heads // group,)),
        dma((heads // group,)),
    ]
    anywhere = pl.BlockSpec(memory_space=pl.ANY)
    inside_vmem = pl.BlockSpec(memory_space=pltpu.VMEM)
    done = pl.pallas_call(
        functools.partial(kernel, sizes),
        in_specs=[pl.BlockSpec(memory_space=pltpu.HBM)] * 4,
        out_specs=[inside_vmem] * len(results),
        out_shape=results,
        scratch_shapes=scratch,
        compiler_params=pltpu.CompilerParams(
            collective_id=0, has_side_effects=True, vmem_limit_bytes=34 * 2**20
        ),
        name="attend",
    )(projected, conv_weight, level_codes, out_gain.reshape(1, width))
    tok_bits = rows.bit_length() - 1
    pieces = ahead * dim // (group * dim)

    def deliver(*refs):
        mixed, given = refs[0], refs[1 : 5 + bits]
        target, fresh, sem = refs[5 + bits :]

        def piece(at):
            lanes = pl.ds(at * group * dim, group * dim)
            return pltpu.make_async_copy(mixed.at[:, lanes], target.at[:, lanes], sem.at[at])

        def rest(at):
            lanes = pl.ds(at * chunk * dim, chunk * dim)
            lies = pl.ds((ahead + at * chunk) * dim, chunk * dim)
            return pltpu.make_async_copy(fresh.at[:, lanes], target.at[:, lies], sem.at[pieces + at])

        for at in range(pieces):
            piece(at).start()
        for at in range(tail):
            heads_here = range(ahead + at * chunk, ahead + (at + 1) * chunk)
            together(
                mix((dim, block, tok_bits + 1), given, fresh, head, lanes_of(head - ahead, dim), part)
                for head in heads_here
                for part in range(rows // block)
            )
            rest(at).start()
        for at in range(pieces):
            piece(at).wait()
        for at in range(tail):
            rest(at).wait()

    return pl.pallas_call(
        deliver,
        in_specs=[inside_vmem] * len(results),
        out_specs=anywhere,
        out_shape=jax.ShapeDtypeStruct((rows, width), BF16),
        scratch_shapes=[vmem((rows, max(1, tail * chunk) * dim), BF16), dma((pieces + tail,))],
        compiler_params=pltpu.CompilerParams(vmem_limit_bytes=4 * 2**20),
        name="deliver",
    )(*done)


def solution(mesh):
    placed = (P(None, ("groups", "ctx"), None), P(), P(None, None, ("groups", "ctx")), P())
    return jax.shard_map(
        on_device, mesh=mesh, in_specs=placed, out_specs=P(("groups", "ctx"), None), check_vma=False
    )
```
